32 devices in a mesh: row: 4 (over y, x), col: 8 (over z, core).
Axes of the slice: x: 2, y: 2, z: 4, core: 2. Of those that a mesh axis runs over, the one named last changes fastest.
Arguments:
- increment: float32 [4, 60, 32, 1024], P(None, None, 'row', 'col'), may hold values from -6 to 6
- residual: float32 [4, 60, 32, 1024], P(None, None, 'row', 'col'), may hold values from -6 to 6
- direction: float32 [4, 60, 32, 1024], P(None, None, 'row', 'col'), may hold values from -6 to 6
- lanczos: bfloat16 [10, 4, 60, 32, 1024], P(None, None, None, 'row', 'col'), may hold values from -10 to 10
- vertical_modes: float32 [4, 60, 60], replicated, may hold values from -0.75 to 0.75
- amplitude: float32 [4, 60], replicated, may hold values from 0.5 to 2
- length_east: float32 [4, 8], replicated, may hold values from 0.25 to 4
- length_north: float32 [4, 8], replicated, may hold values from 0.25 to 4
- observed_cell: int32 [16384], P(('row', 'col')), may hold values from 0 to 245759
- observed_weight: float32 [16384], P(('row', 'col')), may hold values from 0.5 to 4
- observed_count: int32 [32], P(('row', 'col')), may hold values from 128 to 512, as said below
Outputs:
- new_increment: float32 [4, 60, 32, 1024], P(None, None, 'row', 'col')
- new_residual: float32 [4, 60, 32, 1024], P(None, None, 'row', 'col')
- new_direction: float32 [4, 60, 32, 1024], P(None, None, 'row', 'col')
The draws below stay inside these ranges and needn't reach their ends.
Inputs may be any that keep to these rules, and one draw needn't show every extreme that they name: observed_cell[s] indexes a cell of the tile that slot s belongs to. `observed_count`: a tile has at most 512 live slots, and some tile has exactly 512.
All inputs are finite; a program needn't handle non-finite values.
Results may differ from the reference program's by a relative error of at most 0.00055.
Values sent between devices are 32-bit elements; how exact they have to be, the bound alone decides.
A program may use at most 128 MiB of HBM per device.

```python
import math
import jax
import jax.numpy as jnp
from jax import lax

V = 4
L = 60
M = 8
K = 10
CX = 128
CY = 8
OBS_DEV = 512
NX = 1024
NY = 32
TILES = 32
NOBS = 16384
NTOT = 7864320


def shared_residual(key):
    noise_key = jax.random.fold_in(key, 11)
    return jnp.clip(jax.random.normal(noise_key, (V, L, NY, NX), jnp.float32), -6.0, 6.0)


def draw_residual(key, part):
    return shared_residual(key)


def draw_lanczos(key, part):
    base_field = shared_residual(key)
    fresh = jnp.clip(jax.random.normal(jax.random.fold_in(key, 12), (K, V, L, NY, NX), jnp.float32), -6.0, 6.0)
    mixing = 0.2 + 0.04 * jnp.arange(K, dtype=jnp.float32)
    mixed = (fresh + mixing[:, None, None, None, None] * base_field[None]) / jnp.sqrt(1.0 + mixing * mixing)[:, None, None, None, None]
    return mixed.astype(jnp.bfloat16)


def draw_observed_count(key, part):
    count_key = jax.random.fold_in(key, 21)
    place_key = jax.random.fold_in(key, 22)
    counts = jax.random.randint(count_key, (TILES,), OBS_DEV // 4, OBS_DEV + 1)
    chosen = jax.random.randint(place_key, (), 0, TILES)
    return jnp.where(jnp.arange(TILES) == chosen, OBS_DEV, counts).astype(jnp.int32)


def with_ends(values, rng, least, largest):
    place = [jax.random.randint(jax.random.fold_in(rng, axis), (), 0, length) for axis, length in enumerate(values.shape)]
    longest = values.shape.index(max(values.shape))
    next_to = place[:longest] + [(place[longest] + 1) % values.shape[longest]] + place[longest + 1:]
    return values.at[tuple(place)].set(least).at[tuple(next_to)].set(largest)


def block_scale(own_key, extent, cuts, least, largest):
    gain, own = 1.0, jax.random.fold_in(own_key, 6)
    for axis_at, blocks in cuts:
        draws = jnp.exp(jax.random.uniform(jax.random.fold_in(own, axis_at), (blocks,), jnp.float32, least / len(cuts), largest / len(cuts)))
        gain = gain * jnp.repeat(draws, extent[axis_at] // blocks).reshape([-1 if axis == axis_at else 1 for axis in range(len(extent))])
    return gain


def scatter_about(rng, shape, scale, reach, shards=(), held_as=jnp.bfloat16):
    result = scale * jax.random.normal(rng, shape, jnp.float32)
    if shards:
        result = result * block_scale(rng, shape, shards, -0.22, 0.18)
    return jnp.clip(result, -reach, reach).astype(held_as)


def setup_inputs(seed: int = 0) -> dict:
    seeds = jax.random.split(jax.random.key(seed), 12)
    increment = scatter_about(seeds[0], (V, L, NY, NX), 1.0, 6.0, ((2, 4), (3, 8)), jnp.float32)
    residual = draw_residual(jax.random.fold_in(seeds[11], 71), 0)
    direction = scatter_about(seeds[2], (V, L, NY, NX), 1.0, 6.0, ((2, 4), (3, 8)), jnp.float32)
    lanczos = draw_lanczos(jax.random.fold_in(seeds[11], 71), 0)
    vertical_modes = scatter_about(seeds[4], (V, L, L), L ** -0.5, 0.75, (), jnp.float32)
    amplitude = jnp.clip(jnp.exp(jax.random.uniform(seeds[5], (V, L), jnp.float32, math.log(0.5), math.log(2.0))), 0.5, 2.0)
    length_east = jnp.clip(jnp.exp(jax.random.uniform(seeds[6], (V, M), jnp.float32, math.log(0.25), math.log(4.0))), 0.25, 4.0)
    length_north = jnp.clip(jnp.exp(jax.random.uniform(seeds[7], (V, M), jnp.float32, math.log(0.25), math.log(4.0))), 0.25, 4.0)
    observed_cell = with_ends(jax.random.randint(seeds[8], (NOBS,), 0, V * L * CY * CX), jax.random.fold_in(seeds[8], 1), 0, (V * L * CY * CX) - 1).astype(jnp.int32)
    observed_weight = jnp.clip(jnp.exp(math.log(4.0) - 2.0794415 * jax.random.uniform(seeds[9], (NOBS,), jnp.float32) ** block_scale(seeds[9], (NOBS,), ((0, 32),), -0.2, 0.2)), 0.5, 4.0)
    observed_count = draw_observed_count(jax.random.fold_in(seeds[11], 71), 0)
    return {"increment": increment, "residual": residual, "direction": direction, "lanczos": lanczos, "vertical_modes": vertical_modes, "amplitude": amplitude, "length_east": length_east, "length_north": length_north, "observed_cell": observed_cell, "observed_weight": observed_weight, "observed_count": observed_count}


precise = lax.Precision.HIGHEST

def recursive_filter(field_in, alpha_line):
    decay = alpha_line[:, :, None]
    sequence = jnp.moveaxis(field_in, -1, 0)

    def advance(carry_in, entry):
        carry_out = decay * carry_in + (1.0 - decay) * entry
        return (carry_out, carry_out)
    first_state, smooth = lax.scan(advance, jnp.zeros_like(sequence[0]), sequence)
    second_state, settled = lax.scan(advance, jnp.zeros_like(sequence[0]), smooth, reverse=True)
    boost = jnp.sqrt((1.0 + alpha_line) / (1.0 - alpha_line))[:, :, None, None]
    return jnp.moveaxis(settled, 0, -1) * boost

def along_east(leading, alpha_east):
    return recursive_filter(leading, alpha_east)

def along_north(leading, alpha_north):
    return jnp.swapaxes(recursive_filter(jnp.swapaxes(leading, 2, 3), alpha_north), 2, 3)

def reference(increment, residual, direction, lanczos, vertical_modes, amplitude, length_east, length_north, observed_cell, observed_weight, observed_count):
    alpha_east = jnp.exp(-1.0 / (length_east * CX))
    alpha_north = jnp.exp(-1.0 / (length_north * CY))

    def forward_map(control):
        leading = along_north(along_east(control[:, :M], alpha_east), alpha_north)
        mode_field = jnp.concatenate([leading, control[:, M:]], axis=1)
        return jnp.einsum('vlm,vmyx->vlyx', vertical_modes, mode_field * amplitude[:, :, None, None], precision=precise)

    def adjoint_map(grid_field):
        mode_field = jnp.einsum('vlm,vlyx->vmyx', vertical_modes, grid_field, precision=precise) * amplitude[:, :, None, None]
        leading = along_east(along_north(mode_field[:, :M], alpha_north), alpha_east)
        return jnp.concatenate([leading, mode_field[:, M:]], axis=1)
    grid_field = forward_map(direction)
    ytiles = NY // CY
    xtiles = NX // CX
    tiled = grid_field.reshape(V, L, ytiles, CY, xtiles, CX).transpose(2, 4, 0, 1, 3, 5).reshape(ytiles * xtiles, V * L * CY * CX)
    slots = observed_cell.reshape(ytiles * xtiles, OBS_DEV)
    picked = jnp.take_along_axis(tiled, slots, axis=1)
    live_slots = jnp.arange(OBS_DEV)[None, :] < observed_count[:, None]
    weighted = jnp.where(live_slots, observed_weight.reshape(ytiles * xtiles, OBS_DEV) * picked, 0.0)
    tile_rows = jnp.broadcast_to(jnp.arange(ytiles * xtiles)[:, None], slots.shape)
    spread_tiles = jnp.zeros_like(tiled).at[tile_rows, slots].add(weighted)
    spread = spread_tiles.reshape(ytiles, xtiles, V, L, CY, CX).transpose(2, 3, 0, 4, 1, 5).reshape(V, L, NY, NX)
    image = direction + adjoint_map(spread)
    norm_old = jnp.sum(residual * residual)
    curvature = jnp.sum(direction * image)
    step_size = norm_old / curvature
    new_increment = increment + step_size * direction
    moved = residual - step_size * image
    flat_lanczos = lanczos.reshape(K, -1)
    flat_moved = moved.reshape(-1)

    def intersection_one(vector_row):
        return jnp.sum(vector_row.astype(jnp.float32) * flat_moved)
    intersections = lax.map(intersection_one, flat_lanczos)
    coefficient = intersections / NTOT

    def remove_one(vector_index, running):
        return running - coefficient[vector_index] * flat_lanczos[vector_index].astype(jnp.float32)
    new_flat = lax.fori_loop(0, K, remove_one, flat_moved)
    new_residual = new_flat.reshape(moved.shape)
    norm_new = jnp.sum(new_residual * new_residual)
    new_direction = new_residual + norm_new / norm_old * direction
    return (new_increment, new_residual, new_direction)
```

```python
import functools

import jax
import jax.numpy as jnp
from jax import lax
from jax.experimental import pallas as pl
from jax.experimental.pallas import tpu as pltpu
from jax.sharding import PartitionSpec as P

MESH = pl.DeviceIdType.MESH
f32 = jnp.float32
bf16 = jnp.bfloat16
CHUNK = 32


def kernel(
    R, C, V, L, M, K, ny, nx, total_cells,
    dir_ref, tab_ref, vm_ref, amp_ref, cell_ref, wgt_ref, cnt_ref,
    res_hbm, inc_hbm, lz_hbm,
    oinc_hbm, ores_hbm, odir_hbm,
    res_ref, inc_ref, lz_ref, oinc_ref, ores_ref, odir_ref,
    img_ref, lead_ref, mom_ref, hot_ref, wsum_ref,
    es_ref, er_ref, ns_ref, nr_ref, rs_ref, rr_ref,
    load_sem, out_sem, e_ssem, e_rsem, n_ssem, n_rsem, r_ssem, r_rsem,
):
    N = R * C
    I = V * M
    row, col = lax.axis_index("row"), lax.axis_index("col")
    me = row * C + col
    barrier = pltpu.get_barrier_semaphore()

    def place(d):
        peer = lax.rem(me + d, N)
        return (lax.div(peer, C), lax.rem(peer, C))

    def greet(d, carry):
        pl.semaphore_signal(barrier, inc=1, device_id=place(d), device_id_type=MESH)
        return carry

    lax.fori_loop(1, N, greet, 0)
    loads = [
        pltpu.make_async_copy(res_hbm, res_ref, load_sem.at[0]),
        pltpu.make_async_copy(lz_hbm, lz_ref, load_sem.at[1]),
        pltpu.make_async_copy(inc_hbm, inc_ref, load_sem.at[2]),
    ]
    for load in loads:
        load.start()

    lane = lax.broadcasted_iota(jnp.int32, (1, 1, nx), 2)
    sub = lax.broadcasted_iota(jnp.int32, (1, ny, 1), 1)

    def log_alpha(which):
        return tab_ref[which].reshape(I, ny, nx)

    def scans(u, which):
        axis, size, at = ((2, nx, lane), (1, ny, sub))[which]
        power = jnp.exp(log_alpha(which))
        f, g = u, u
        shift = 1
        while shift < size:
            f = f + power * jnp.where(at >= shift, pltpu.roll(f, shift, axis), 0.0)
            g = g + power * jnp.where(at < size - shift, pltpu.roll(g, size - shift, axis), 0.0)
            power = power * power
            shift *= 2
        return f, g

    def combine(first, second, log_small, index, count, size, own, received):
        at = index.astype(f32)
        left = jnp.zeros_like(log_small)
        right = jnp.zeros_like(log_small)
        edge = jnp.zeros_like(log_small)
        for d in range(count):
            e, b, e_edge = own if d == 0 else received(d)
            wraps = d > index
            source = jnp.where(wraps, index - d + count, index - d).astype(f32)
            if d > 0:
                left += jnp.where(wraps, 0.0, jnp.exp(log_small * float(size * (d - 1)))) * e
                right += jnp.where(wraps, jnp.exp(log_small * float(size * (count - d - 1))), 0.0) * b
            edge += jnp.exp(log_small * (float(size * (count - 1)) - size * source + 1.0)) * e_edge
        right -= jnp.exp(log_small * (size * (float(count - 1) - at))) * edge
        return left, right

    def line_scale(which):
        a = jnp.exp(log_alpha(which))
        return jnp.sqrt((1.0 - a) / (1.0 + a))

    def east_copies(inst):
        return [
            pltpu.make_async_remote_copy(
                src_ref=es_ref.at[inst],
                dst_ref=er_ref.at[inst, d],
                send_sem=e_ssem.at[inst, d],
                recv_sem=e_rsem.at[inst, d],
                device_id=(row, lax.rem(col + d, C)),
                device_id_type=MESH,
            )
            for d in range(1, C)
        ]

    def north_copies(inst):
        return [
            pltpu.make_async_remote_copy(
                src_ref=ns_ref.at[inst],
                dst_ref=nr_ref.at[inst, d],
                send_sem=n_ssem.at[inst, d],
                recv_sem=n_rsem.at[inst, d],
                device_id=(lax.rem(row + d, R), col),
                device_id_type=MESH,
            )
            for d in range(1, R)
        ]

    small_lane = lax.broadcasted_iota(jnp.int32, (ny, nx), 1)

    def east_start(u, inst):
        f, g = scans(u, 0)
        first = jnp.zeros((ny, nx), f32)
        second = jnp.zeros((ny, nx), f32)
        for i in range(I):
            e = jnp.broadcast_to(f[i, :, nx - 1 : nx], (ny, nx))
            b = jnp.broadcast_to(g[i, :, 0:1], (ny, nx))
            first = jnp.where(small_lane == i, e, first)
            first = jnp.where(small_lane == I + i, b, first)
            second = jnp.where(small_lane == I + i, e, second)
        es_ref[inst, 0] = first
        es_ref[inst, 1] = second
        lead_ref[...] = (f + g - u).reshape(I * ny, nx)
        return east_copies(inst)

    def east_finish(inst, copies):
        for copy in copies:
            copy.wait()
        log_small = jnp.zeros((ny, nx), f32)
        for i in range(I):
            hit = (small_lane == i) | (small_lane == I + i)
            log_small = jnp.where(hit, tab_ref[0, i * ny : (i + 1) * ny, :], log_small)
        left, right = combine(
            None, None, log_small, col, C, nx,
            (es_ref[inst, 0], es_ref[inst, 0], es_ref[inst, 1]),
            lambda d: (er_ref[inst, d, 0], er_ref[inst, d, 0], er_ref[inst, d, 1]),
        )
        at = lax.broadcasted_iota(jnp.int32, (ny, nx), 1).astype(f32)
        for i in range(I):
            rows = slice(i * ny, (i + 1) * ny)
            log_a = tab_ref[0, rows, :]
            x = jnp.broadcast_to(left[:, i : i + 1], (ny, nx))
            y = jnp.broadcast_to(right[:, I + i : I + i + 1], (ny, nx))
            a = jnp.exp(log_a)
            lead_ref[rows, :] = jnp.sqrt((1.0 - a) / (1.0 + a)) * (
                lead_ref[rows, :]
                + jnp.exp(log_a * (at + 1.0)) * x
                + jnp.exp(log_a * (float(nx) - at)) * y
            )

    def north_start(u, inst):
        f, g = scans(u, 1)
        mom_ref[0] = f.reshape(I * ny, nx)
        mom_ref[1] = g.reshape(I * ny, nx)
        ns_ref[inst, 0] = mom_ref[0, pl.ds(ny - 1, I, stride=ny), :]
        ns_ref[inst, 1] = mom_ref[1, pl.ds(0, I, stride=ny), :]
        lead_ref[...] = (f + g - u).reshape(I * ny, nx)
        return north_copies(inst)

    def north_finish(inst, copies):
        for copy in copies:
            copy.wait()
        log_small = tab_ref[1, pl.ds(0, I, stride=ny), :]
        left, right = combine(
            None, None, log_small, row, R, ny,
            (ns_ref[inst, 0], ns_ref[inst, 1], ns_ref[inst, 0]),
            lambda d: (nr_ref[inst, d, 0], nr_ref[inst, d, 1], nr_ref[inst, d, 0]),
        )
        at = lax.broadcasted_iota(jnp.int32, (ny, nx), 0).astype(f32)
        for i in range(I):
            rows = slice(i * ny, (i + 1) * ny)
            log_a = tab_ref[1, rows, :]
            x = jnp.broadcast_to(left[i : i + 1, :], (ny, nx))
            y = jnp.broadcast_to(right[i : i + 1, :], (ny, nx))
            a = jnp.exp(log_a)
            lead_ref[rows, :] = jnp.sqrt((1.0 - a) / (1.0 + a)) * (
                lead_ref[rows, :]
                + jnp.exp(log_a * (at + 1.0)) * x
                + jnp.exp(log_a * (float(ny) - at)) * y
            )

    plane = L * ny
    u = jnp.concatenate([dir_ref[v * plane : v * plane + M * ny, :] for v in range(V)], axis=0)
    copies = east_start(u.reshape(I, ny, nx), 0)
    pl.semaphore_wait(barrier, N - 1)
    for copy in copies:
        copy.start()

    cell = cell_ref[...]
    slots = cell.shape[1]
    level = lax.shift_right_logical(cell, (ny * nx).bit_length() - 1)
    spot = cell & (ny * nx - 1)
    hot_ref[...] = jnp.where(
        lax.broadcasted_iota(jnp.int32, (ny * nx, slots), 0) == spot, 1.0, 0.0
    ).astype(bf16)
    live = lax.broadcasted_iota(jnp.int32, (1, slots), 1) < cnt_ref[0]
    weight = jnp.where(live, wgt_ref[...], 0.0)
    parts = []
    rest = weight
    for _ in range(3):
        part = rest.astype(bf16).astype(f32)
        parts.append(part)
        rest = rest - part
    nt = (((1,), (1,)), ((), ()))
    for v in range(V):
        hit = lax.broadcasted_iota(jnp.int32, (L, slots), 0) + v * L == level
        wsum_ref[v] = sum(
            lax.dot_general(
                jnp.where(hit, part, 0.0).astype(bf16), hot_ref[...], nt,
                preferred_element_type=f32,
            )
            for part in parts
        )

    east_finish(0, copies)
    copies = north_start(lead_ref[...].reshape(I, ny, nx), 0)
    for copy in copies:
        copy.start()
    north_finish(0, copies)

    for v in range(V):
        mixed = vm_ref[v] * amp_ref[v : v + 1, :]
        field = jnp.concatenate(
            [
                jnp.concatenate(
                    [
                        lead_ref[pl.ds(v * M * ny + y, M, stride=ny), :],
                        dir_ref[pl.ds(v * plane + M * ny + y, L - M, stride=ny), :],
                    ],
                    axis=0,
                )
                for y in range(ny)
            ],
            axis=1,
        )
        grid = lax.dot_general(
            mixed, field, (((1,), (0,)), ((), ())),
            precision=lax.Precision.HIGHEST, preferred_element_type=f32,
        )
        spread = grid * wsum_ref[v]
        back = lax.dot_general(
            mixed.T, spread, (((1,), (0,)), ((), ())),
            precision=lax.Precision.HIGHEST, preferred_element_type=f32,
        )
        for y in range(ny):
            img_ref[pl.ds(v * plane + y, L, stride=ny), :] = back[:, y * nx : (y + 1) * nx]

    u = jnp.concatenate([img_ref[v * plane : v * plane + M * ny, :] for v in range(V)], axis=0)
    copies = north_start(u.reshape(I, ny, nx), 1)
    for copy in copies:
        copy.start()

    steps = V * plane // CHUNK

    def fold(x):
        return jnp.sum(x.reshape(CHUNK // 8, 8, nx), axis=0)

    loads[0].wait()
    loads[1].wait()
    zero = jnp.zeros((8, nx), f32)

    def first_dots(s, carry):
        rows = pl.ds(pl.multiple_of(s * CHUNK, CHUNK), CHUNK)
        r = res_ref[rows, :]
        out = [carry[0] + fold(r * r)]
        for k in range(K):
            out.append(carry[k + 1] + fold(r * lz_ref[k, rows, :].astype(f32)))
        return tuple(out)

    res_dots = lax.fori_loop(0, steps, first_dots, (zero,) * (K + 1))

    north_finish(1, copies)
    copies = east_start(lead_ref[...].reshape(I, ny, nx), 1)
    for copy in copies:
        copy.start()
    east_finish(1, copies)
    for v in range(V):
        img_ref[v * plane : v * plane + M * ny, :] = lead_ref[v * M * ny : (v + 1) * M * ny, :]

    def second_dots(s, carry):
        rows = pl.ds(pl.multiple_of(s * CHUNK, CHUNK), CHUNK)
        d = dir_ref[rows, :]
        image = d + img_ref[rows, :]
        img_ref[rows, :] = image
        out = [carry[0] + fold(d * image)]
        for k in range(K):
            out.append(carry[k + 1] + fold(image * lz_ref[k, rows, :].astype(f32)))
        return tuple(out)

    img_dots = lax.fori_loop(0, steps, second_dots, (zero,) * (K + 1))

    def reduce_copy(inst, d):
        return pltpu.make_async_remote_copy(
            src_ref=rs_ref.at[inst],
            dst_ref=rr_ref.at[inst, d],
            send_sem=r_ssem.at[inst, d],
            recv_sem=r_rsem.at[inst, d],
            device_id=place(d),
            device_id_type=MESH,
        )

    def reduce_start(inst):
        def go(d, carry):
            reduce_copy(inst, d).start()
            return carry

        lax.fori_loop(1, N, go, 0)

    def reduce_finish(inst):
        def go(d, carry):
            reduce_copy(inst, d).wait()
            return carry

        lax.fori_loop(1, N, go, 0)
        rr_ref[inst, 0] = rs_ref[inst]
        return jnp.sum(rr_ref[inst], axis=0)

    sums = list(res_dots) + list(img_dots)
    small_sub = lax.broadcasted_iota(jnp.int32, (8, nx), 0)
    packed = zero
    for n, part in enumerate(sums):
        here = (small_sub == n % 8) & (small_lane == n // 8)
        packed = jnp.where(here, jnp.sum(part, axis=(0, 1), keepdims=True), packed)
    rs_ref[0] = packed
    reduce_start(0)
    loads[2].wait()
    totals = reduce_finish(0)

    def total(n):
        return totals[n % 8 : n % 8 + 1, n // 8 : n // 8 + 1]

    norm_old = total(0)
    step_size = norm_old / total(K + 1)
    coefficient = [
        jnp.broadcast_to((total(k + 1) - step_size * total(K + 2 + k)) / total_cells, (CHUNK, nx))
        for k in range(K)
    ]
    step_wide = jnp.broadcast_to(step_size, (CHUNK, nx))

    def update(s, carry):
        rows = pl.ds(pl.multiple_of(s * CHUNK, CHUNK), CHUNK)
        oinc_ref[rows, :] = inc_ref[rows, :] + step_wide * dir_ref[rows, :]
        moved = res_ref[rows, :] - step_wide * img_ref[rows, :]
        for k in range(K):
            moved = moved - coefficient[k] * lz_ref[k, rows, :].astype(f32)
        ores_ref[rows, :] = moved
        return carry + fold(moved * moved)

    norm_part = lax.fori_loop(0, steps, update, zero)
    rs_ref[1] = jnp.broadcast_to(jnp.sum(norm_part, axis=(0, 1), keepdims=True), (8, nx))
    reduce_start(1)
    stores = [
        pltpu.make_async_copy(oinc_ref, oinc_hbm, out_sem.at[0]),
        pltpu.make_async_copy(ores_ref, ores_hbm, out_sem.at[1]),
        pltpu.make_async_copy(odir_ref, odir_hbm, out_sem.at[2]),
    ]
    stores[0].start()
    stores[1].start()
    ratio = jnp.broadcast_to(reduce_finish(1)[0:1, 0:1] / norm_old, (CHUNK, nx))

    def turn(s, carry):
        rows = pl.ds(pl.multiple_of(s * CHUNK, CHUNK), CHUNK)
        odir_ref[rows, :] = ores_ref[rows, :] + ratio * dir_ref[rows, :]
        return carry

    lax.fori_loop(0, steps, turn, 0)
    stores[2].start()
    for store in stores:
        store.wait()


def local(
    R, C,
    increment, residual, direction, lanczos, vertical_modes, amplitude,
    length_east, length_north, observed_cell, observed_weight, observed_count,
):
    V, L, ny, nx = direction.shape
    M = length_east.shape[1]
    K = lanczos.shape[0]
    I = V * M
    N = R * C
    flat = V * L * ny
    slots = observed_cell.shape[0]
    logs = jnp.stack([-1.0 / (length_east * nx), -1.0 / (length_north * ny)])
    table = jnp.broadcast_to(logs.reshape(2, I, 1, 1), (2, I, ny, nx)).reshape(2, I * ny, nx)
    vmem = pl.BlockSpec(memory_space=pltpu.VMEM)
    hbm = pl.BlockSpec(memory_space=pl.ANY)
    smem = pl.BlockSpec(memory_space=pltpu.SMEM)
    field = jax.ShapeDtypeStruct((flat, nx), f32)
    big = pltpu.VMEM((flat, nx), f32)
    out = pl.pallas_call(
        functools.partial(kernel, R, C, V, L, M, K, ny, nx, float(flat * nx * N)),
        out_shape=(field,) * 3,
        in_specs=[vmem] * 6 + [smem] + [hbm] * 3,
        out_specs=(hbm,) * 3,
        scratch_shapes=[
            big, big, pltpu.VMEM((K, flat, nx), bf16), big, big, big,
            big, pltpu.VMEM((I * ny, nx), f32), pltpu.VMEM((2, I * ny, nx), f32),
            pltpu.VMEM((ny * nx, slots), bf16), pltpu.VMEM((V, L, ny * nx), f32),
            pltpu.VMEM((2, 2, ny, nx), f32), pltpu.VMEM((2, C, 2, ny, nx), f32),
            pltpu.VMEM((2, 2, I, nx), f32), pltpu.VMEM((2, R, 2, I, nx), f32),
            pltpu.VMEM((2, 8, nx), f32), pltpu.VMEM((2, N, 8, nx), f32),
            pltpu.SemaphoreType.DMA((3,)), pltpu.SemaphoreType.DMA((3,)),
            pltpu.SemaphoreType.DMA((2, C)), pltpu.SemaphoreType.DMA((2, C)),
            pltpu.SemaphoreType.DMA((2, R)), pltpu.SemaphoreType.DMA((2, R)),
            pltpu.SemaphoreType.DMA((2, N)), pltpu.SemaphoreType.DMA((2, N)),
        ],
        compiler_params=pltpu.CompilerParams(
            collective_id=0, has_side_effects=True, vmem_limit_bytes=48 * 2**20
        ),
    )(
        direction.reshape(flat, nx), table, vertical_modes, amplitude,
        observed_cell.reshape(1, slots), observed_weight.reshape(1, slots), observed_count,
        residual.reshape(flat, nx), increment.reshape(flat, nx), lanczos.reshape(K, flat, nx),
    )
    return tuple(x.reshape(direction.shape) for x in out)


def solution(mesh):
    field = P(None, None, "row", "col")
    tile = P(("row", "col"))
    in_specs = (
        field, field, field, P(None, None, None, "row", "col"),
        P(), P(), P(), P(), tile, tile, tile,
    )
    return jax.shard_map(
        functools.partial(local, mesh.shape["row"], mesh.shape["col"]),
        mesh=mesh, in_specs=in_specs, out_specs=(field,) * 3, check_vma=False,
    )
```

```python
import functools

import jax
import jax.numpy as jnp
from jax import lax
from jax.experimental import pallas as pl
from jax.experimental.pallas import tpu as pltpu
from jax.sharding import PartitionSpec as P

MESH = pl.DeviceIdType.MESH
f32 = jnp.float32
bf16 = jnp.bfloat16
CHUNK = 32


def kernel(
    R, C, V, L, M, K, ny, nx, total_cells,
    cnt_ref, dir_hbm, len_e_hbm, len_n_hbm, vm_hbm, amp_hbm, cell_hbm, wgt_hbm,
    res_hbm, inc_hbm, lz_hbm,
    oinc_all, ores_all, odir_all,
    dir_ref, len_ref, vm_ref, amp_ref, cell_ref, wgt_ref,
    tab_ref, own_ref, near_ref, far_ref, mix_ref,
    res_ref, inc_ref, lz_ref,
    img_ref, lead_ref, mom_ref, hot_ref, wsum_ref,
    es_ref, er_ref, ns_ref, nr_ref, rs_ref, rr_ref,
    load_sem, e_ssem, e_rsem, n_ssem, n_rsem, r_ssem, r_rsem,
):
    N = R * C
    I = V * M
    oinc_ref, ores_ref, odir_ref = (
        x.reshape(V * L * ny, nx) for x in (oinc_all, ores_all, odir_all)
    )
    row, col = lax.axis_index("row"), lax.axis_index("col")
    me = row * C + col
    barrier = pltpu.get_barrier_semaphore()

    def place(d):
        peer = lax.rem(me + d, N)
        return (lax.div(peer, C), lax.rem(peer, C))

    def greet(d, carry):
        pl.semaphore_signal(barrier, inc=1, device_id=place(d), device_id_type=MESH)
        return carry

    plane = L * ny
    lead_rows = M * ny
    firsts = [
        pltpu.make_async_copy(len_e_hbm, len_ref.at[0], load_sem.at[3]),
        pltpu.make_async_copy(len_n_hbm, len_ref.at[1], load_sem.at[4]),
    ]
    others = [
        pltpu.make_async_copy(cell_hbm, cell_ref, load_sem.at[5]),
        pltpu.make_async_copy(wgt_hbm, wgt_ref, load_sem.at[6]),
        pltpu.make_async_copy(vm_hbm, vm_ref, load_sem.at[7]),
        pltpu.make_async_copy(amp_hbm, amp_ref, load_sem.at[8]),
    ]
    for v in range(V):
        part = pl.ds(v * plane, lead_rows)
        firsts.append(
            pltpu.make_async_copy(dir_hbm.at[part], dir_ref.at[part], load_sem.at[9 + v])
        )
        part = pl.ds(v * plane + lead_rows, plane - lead_rows)
        others.append(
            pltpu.make_async_copy(dir_hbm.at[part], dir_ref.at[part], load_sem.at[9 + V + v])
        )
    loads = [
        pltpu.make_async_copy(res_hbm, res_ref, load_sem.at[0]),
        pltpu.make_async_copy(lz_hbm, lz_ref, load_sem.at[1]),
        pltpu.make_async_copy(inc_hbm, inc_ref, load_sem.at[2]),
    ]
    for load in firsts + others + loads:
        load.start()
    lax.fori_loop(1, N, greet, 0)
    for load in firsts:
        load.wait()
    for i in range(I):
        v, m = i // M, i % M
        rows = slice(i * ny, (i + 1) * ny)
        for which, size in ((0, nx), (1, ny)):
            length = jnp.broadcast_to(len_ref[which, v : v + 1, m : m + 1], (ny, nx))
            tab_ref[which, rows, :] = -1.0 / (length * float(size))

    lane = lax.broadcasted_iota(jnp.int32, (1, 1, nx), 2)
    sub = lax.broadcasted_iota(jnp.int32, (1, ny, 1), 1)

    def log_alpha(which):
        return tab_ref[which].reshape(I, ny, nx)

    def scans(u, which):
        axis, size, at = ((2, nx, lane), (1, ny, sub))[which]
        power = jnp.exp(log_alpha(which))
        f, g = u, u
        shift = 1
        while shift < size:
            f = f + power * jnp.where(at >= shift, pltpu.roll(f, shift, axis), 0.0)
            g = g + power * jnp.where(at < size - shift, pltpu.roll(g, size - shift, axis), 0.0)
            power = power * power
            shift *= 2
        return f, g

    def weights(log_small, index, count, size):
        at = index.astype(f32)
        left, right, edge = [None], [None], []
        back = jnp.exp(log_small * (size * (float(count - 1) - at)))
        for d in range(count):
            wraps = d > index
            source = jnp.where(wraps, index - d + count, index - d).astype(f32)
            if d > 0:
                left.append(jnp.where(wraps, 0.0, jnp.exp(log_small * float(size * (d - 1)))))
                right.append(
                    jnp.where(wraps, jnp.exp(log_small * float(size * (count - d - 1))), 0.0)
                )
            edge.append(
                back * jnp.exp(log_small * (float(size * (count - 1)) - size * source + 1.0))
            )
        return left, right, edge

    def combine(table, own, received, copies):
        left_w, right_w, edge_w = table
        e, b, e_edge = own
        left = jnp.zeros_like(e)
        right = -edge_w[0] * e_edge
        for d, copy in enumerate(copies, 1):
            copy.wait_recv()
            e, b, e_edge = received(d)
            left += left_w[d] * e
            right += right_w[d] * b - edge_w[d] * e_edge
        for copy in copies:
            copy.wait_send()
        return left, right

    def tables(which):
        size, at = ((nx, lane), (ny, sub))[which]
        log_a = log_alpha(which)
        a = jnp.exp(log_a)
        scale = jnp.sqrt((1.0 - a) / (1.0 + a))
        at = at.astype(f32)
        own_ref[which] = scale.reshape(I * ny, nx)
        near_ref[which] = (scale * jnp.exp(log_a * (at + 1.0))).reshape(I * ny, nx)
        far_ref[which] = (scale * jnp.exp(log_a * (float(size) - at))).reshape(I * ny, nx)

    def east_copies(inst):
        return [
            pltpu.make_async_remote_copy(
                src_ref=es_ref.at[inst],
                dst_ref=er_ref.at[inst, d],
                send_sem=e_ssem.at[inst, d],
                recv_sem=e_rsem.at[inst, d],
                device_id=(row, lax.rem(col + d, C)),
                device_id_type=MESH,
            )
            for d in range(1, C)
        ]

    def north_copies(inst):
        return [
            pltpu.make_async_remote_copy(
                src_ref=ns_ref.at[inst],
                dst_ref=nr_ref.at[inst, d],
                send_sem=n_ssem.at[inst, d],
                recv_sem=n_rsem.at[inst, d],
                device_id=(lax.rem(row + d, R), col),
                device_id_type=MESH,
            )
            for d in range(1, R)
        ]

    small_lane = lax.broadcasted_iota(jnp.int32, (ny, nx), 1)

    def east_start(u, inst):
        f, g = scans(u, 0)
        first = jnp.zeros((ny, nx), f32)
        second = jnp.zeros((ny, nx), f32)
        for i in range(I):
            e = jnp.broadcast_to(f[i, :, nx - 1 : nx], (ny, nx))
            b = jnp.broadcast_to(g[i, :, 0:1], (ny, nx))
            first = jnp.where(small_lane == i, e, first)
            first = jnp.where(small_lane == I + i, b, first)
            second = jnp.where(small_lane == I + i, e, second)
        es_ref[inst, 0] = first
        es_ref[inst, 1] = second
        lead_ref[...] = (f + g - u).reshape(I * ny, nx)
        return east_copies(inst)

    def east_finish(inst, copies):
        left, right = combine(
            east_table,
            (es_ref[inst, 0], es_ref[inst, 0], es_ref[inst, 1]),
            lambda d: (er_ref[inst, d, 0], er_ref[inst, d, 0], er_ref[inst, d, 1]),
            copies,
        )
        for i in range(I):
            rows = slice(i * ny, (i + 1) * ny)
            x = jnp.broadcast_to(left[:, i : i + 1], (ny, nx))
            y = jnp.broadcast_to(right[:, I + i : I + i + 1], (ny, nx))
            lead_ref[rows, :] = (
                own_ref[0, rows, :] * lead_ref[rows, :]
                + near_ref[0, rows, :] * x
                + far_ref[0, rows, :] * y
            )

    def north_start(u, inst):
        f, g = scans(u, 1)
        mom_ref[0] = f.reshape(I * ny, nx)
        mom_ref[1] = g.reshape(I * ny, nx)
        ns_ref[inst, 0] = mom_ref[0, pl.ds(ny - 1, I, stride=ny), :]
        ns_ref[inst, 1] = mom_ref[1, pl.ds(0, I, stride=ny), :]
        lead_ref[...] = (f + g - u).reshape(I * ny, nx)
        return north_copies(inst)

    def north_finish(inst, copies):
        left, right = combine(
            north_table,
            (ns_ref[inst, 0], ns_ref[inst, 1], ns_ref[inst, 0]),
            lambda d: (nr_ref[inst, d, 0], nr_ref[inst, d, 1], nr_ref[inst, d, 0]),
            copies,
        )
        for i in range(I):
            rows = slice(i * ny, (i + 1) * ny)
            x = jnp.broadcast_to(left[i : i + 1, :], (ny, nx))
            y = jnp.broadcast_to(right[i : i + 1, :], (ny, nx))
            lead_ref[rows, :] = (
                own_ref[1, rows, :] * lead_ref[rows, :]
                + near_ref[1, rows, :] * x
                + far_ref[1, rows, :] * y
            )

    u = jnp.concatenate([dir_ref[v * plane : v * plane + M * ny, :] for v in range(V)], axis=0)
    copies = east_start(u.reshape(I, ny, nx), 0)
    pl.semaphore_wait(barrier, N - 1)
    for copy in copies:
        copy.start()

    log_small = jnp.zeros((ny, nx), f32)
    for i in range(I):
        hit = (small_lane == i) | (small_lane == I + i)
        log_small = jnp.where(hit, tab_ref[0, i * ny : (i + 1) * ny, :], log_small)
    east_table = weights(log_small, col, C, nx)
    tables(0)
    for load in others:
        load.wait()

    pad = mix_ref.shape[1] // 2
    cell = cell_ref[...]
    slots = cell.shape[1]
    level = lax.shift_right_logical(cell, (ny * nx).bit_length() - 1)
    spot = cell & (ny * nx - 1)
    hot_ref[...] = jnp.where(
        lax.broadcasted_iota(jnp.int32, (ny * nx, slots), 0) == spot, 1.0, 0.0
    ).astype(bf16)
    live = lax.broadcasted_iota(jnp.int32, (1, slots), 1) < cnt_ref[0]
    rest = jnp.where(live, wgt_ref[...], 0.0)
    at = lax.broadcasted_iota(jnp.int32, (pad, slots), 0)
    hits = [(at + v * L == level) & (at < L) for v in range(V)]
    lhs = []
    for _ in range(3):
        part = rest.astype(bf16).astype(f32)
        lhs += [jnp.where(hit, part, 0.0).astype(bf16) for hit in hits]
        rest = rest - part
    summed = lax.dot_general(
        jnp.concatenate(lhs, axis=0), hot_ref[...], (((1,), (1,)), ((), ())),
        preferred_element_type=f32,
    )
    for v in range(V):
        wsum_ref[v] = sum(
            summed[(n * V + v) * pad : (n * V + v + 1) * pad] for n in range(3)
        )
    mix_ref[...] = jnp.zeros_like(mix_ref)
    for v in range(V):
        mix_ref[v, 0:L, 0:L] = vm_ref[:, v, :] * amp_ref[v : v + 1, :]

    east_finish(0, copies)
    copies = north_start(lead_ref[...].reshape(I, ny, nx), 0)
    for copy in copies:
        copy.start()
    north_table = weights(tab_ref[1, pl.ds(0, I, stride=ny), :], row, R, ny)
    tables(1)

    def split(x):
        high = x.astype(bf16)
        return high, (x - high.astype(f32)).astype(bf16)

    def wide(x):
        high = x.astype(bf16).astype(f32)
        low = x - high
        return jnp.concatenate(
            [high + pltpu.roll(low, pad, 1), high], axis=1
        )[0:pad, :].astype(bf16)

    def tall(x):
        high, low = split(x)
        return jnp.concatenate([high, high, low, jnp.zeros_like(low)], axis=0)

    sides = []
    for v in range(V):
        mixed = mix_ref[v]
        sides.append((wide(mixed), wide(mixed.T)))
    north_finish(0, copies)

    spare = jnp.zeros((pad - L, nx), f32)
    for v in range(V):
        field = jnp.concatenate(
            [
                jnp.concatenate(
                    [
                        lead_ref[pl.ds(v * lead_rows + y, M, stride=ny), :],
                        dir_ref[pl.ds(v * plane + lead_rows + y, L - M, stride=ny), :],
                        spare,
                    ],
                    axis=0,
                )
                for y in range(ny)
            ],
            axis=1,
        )
        grid = jnp.dot(sides[v][0], tall(field), preferred_element_type=f32)
        back = jnp.dot(sides[v][1], tall(grid * wsum_ref[v]), preferred_element_type=f32)
        for y in range(ny):
            img_ref[pl.ds(v * plane + y, L, stride=ny), :] = back[0:L, y * nx : (y + 1) * nx]

    u = jnp.concatenate([img_ref[v * plane : v * plane + M * ny, :] for v in range(V)], axis=0)
    copies = north_start(u.reshape(I, ny, nx), 1)
    for copy in copies:
        copy.start()

    steps = V * plane // CHUNK

    def fold(x):
        return jnp.sum(x.reshape(CHUNK // 8, 8, nx), axis=0)

    loads[0].wait()
    loads[1].wait()
    zero = jnp.zeros((8, nx), f32)

    def first_dots(s, carry):
        rows = pl.ds(pl.multiple_of(s * CHUNK, CHUNK), CHUNK)
        r = res_ref[rows, :]
        out = [carry[0] + fold(r * r)]
        for k in range(K):
            out.append(carry[k + 1] + fold(r * lz_ref[k, rows, :].astype(f32)))
        return tuple(out)

    res_dots = lax.fori_loop(0, steps, first_dots, (zero,) * (K + 1))

    north_finish(1, copies)
    copies = east_start(lead_ref[...].reshape(I, ny, nx), 1)
    for copy in copies:
        copy.start()
    east_finish(1, copies)
    for v in range(V):
        img_ref[v * plane : v * plane + M * ny, :] = lead_ref[v * M * ny : (v + 1) * M * ny, :]

    def second_dots(s, carry):
        rows = pl.ds(pl.multiple_of(s * CHUNK, CHUNK), CHUNK)
        d = dir_ref[rows, :]
        image = d + img_ref[rows, :]
        img_ref[rows, :] = image
        out = [carry[0] + fold(d * image)]
        for k in range(K):
            out.append(carry[k + 1] + fold(image * lz_ref[k, rows, :].astype(f32)))
        return tuple(out)

    img_dots = lax.fori_loop(0, steps, second_dots, (zero,) * (K + 1))

    def reduce_copy(inst, d):
        return pltpu.make_async_remote_copy(
            src_ref=rs_ref.at[inst],
            dst_ref=rr_ref.at[inst, d],
            send_sem=r_ssem.at[inst, d],
            recv_sem=r_rsem.at[inst, d],
            device_id=place(d),
            device_id_type=MESH,
        )

    def reduce_start(inst):
        def go(d, carry):
            reduce_copy(inst, d).start()
            return carry

        lax.fori_loop(1, N, go, 0)

    def reduce_finish(inst):
        def go(d, carry):
            reduce_copy(inst, d).wait()
            return carry

        lax.fori_loop(1, N, go, 0)
        rr_ref[inst, 0] = rs_ref[inst]
        return jnp.sum(rr_ref[inst], axis=0)

    sums = list(res_dots) + list(img_dots)
    small_sub = lax.broadcasted_iota(jnp.int32, (8, nx), 0)
    packed = zero
    for n, part in enumerate(sums):
        here = (small_sub == n % 8) & (small_lane == n // 8)
        packed = jnp.where(here, jnp.sum(part, axis=(0, 1), keepdims=True), packed)
    rs_ref[0] = packed
    reduce_start(0)
    loads[2].wait()
    totals = reduce_finish(0)

    def total(n):
        return totals[n % 8 : n % 8 + 1, n // 8 : n // 8 + 1]

    norm_old = total(0)
    step_size = norm_old / total(K + 1)
    coefficient = [
        jnp.broadcast_to((total(k + 1) - step_size * total(K + 2 + k)) / total_cells, (CHUNK, nx))
        for k in range(K)
    ]
    step_wide = jnp.broadcast_to(step_size, (CHUNK, nx))

    def update(s, carry):
        rows = pl.ds(pl.multiple_of(s * CHUNK, CHUNK), CHUNK)
        oinc_ref[rows, :] = inc_ref[rows, :] + step_wide * dir_ref[rows, :]
        moved = res_ref[rows, :] - step_wide * img_ref[rows, :]
        for k in range(K):
            moved = moved - coefficient[k] * lz_ref[k, rows, :].astype(f32)
        ores_ref[rows, :] = moved
        return carry + fold(moved * moved)

    norm_part = lax.fori_loop(0, steps, update, zero)
    rs_ref[1] = jnp.broadcast_to(jnp.sum(norm_part, axis=(0, 1), keepdims=True), (8, nx))
    reduce_start(1)
    ratio = jnp.broadcast_to(reduce_finish(1)[0:1, 0:1] / norm_old, (CHUNK, nx))

    def turn(s, carry):
        rows = pl.ds(pl.multiple_of(s * CHUNK, CHUNK), CHUNK)
        odir_ref[rows, :] = ores_ref[rows, :] + ratio * dir_ref[rows, :]
        return carry

    lax.fori_loop(0, steps, turn, 0)


def local(
    R, C,
    increment, residual, direction, lanczos, vertical_modes, amplitude,
    length_east, length_north, observed_cell, observed_weight, observed_count,
):
    V, L, ny, nx = direction.shape
    M = length_east.shape[1]
    K = lanczos.shape[0]
    I = V * M
    N = R * C
    flat = V * L * ny
    slots = observed_cell.shape[0]
    pad = (L + 15) // 16 * 16
    hbm = pl.BlockSpec(memory_space=pltpu.HBM)
    smem = pl.BlockSpec(memory_space=pltpu.SMEM)
    field = pltpu.VMEM((V, L, ny, nx), f32)
    near = pl.BlockSpec(memory_space=pltpu.VMEM)
    big = pltpu.VMEM((flat, nx), f32)
    out = pl.pallas_call(
        functools.partial(kernel, R, C, V, L, M, K, ny, nx, float(flat * nx * N)),
        out_shape=(field,) * 3,
        in_specs=[smem] + [hbm] * 10,
        out_specs=(near,) * 3,
        scratch_shapes=[
            big, pltpu.VMEM((2, V, M), f32), pltpu.VMEM((L, V, L), f32),
            pltpu.VMEM((V, L), f32), pltpu.VMEM((1, slots), jnp.int32), pltpu.VMEM((1, slots), f32),
            pltpu.VMEM((2, I * ny, nx), f32), pltpu.VMEM((2, I * ny, nx), f32),
            pltpu.VMEM((2, I * ny, nx), f32), pltpu.VMEM((2, I * ny, nx), f32),
            pltpu.VMEM((V, 2 * pad, 2 * pad), f32),
            big, big, pltpu.VMEM((K, flat, nx), bf16),
            big, pltpu.VMEM((I * ny, nx), f32), pltpu.VMEM((2, I * ny, nx), f32),
            pltpu.VMEM((ny * nx, slots), bf16), pltpu.VMEM((V, pad, ny * nx), f32),
            pltpu.VMEM((2, 2, ny, nx), f32), pltpu.VMEM((2, C, 2, ny, nx), f32),
            pltpu.VMEM((2, 2, I, nx), f32), pltpu.VMEM((2, R, 2, I, nx), f32),
            pltpu.VMEM((2, 8, nx), f32), pltpu.VMEM((2, N, 8, nx), f32),
            pltpu.SemaphoreType.DMA((9 + 2 * V,)),
            pltpu.SemaphoreType.DMA((2, C)), pltpu.SemaphoreType.DMA((2, C)),
            pltpu.SemaphoreType.DMA((2, R)), pltpu.SemaphoreType.DMA((2, R)),
            pltpu.SemaphoreType.DMA((2, N)), pltpu.SemaphoreType.DMA((2, N)),
        ],
        compiler_params=pltpu.CompilerParams(
            collective_id=0, has_side_effects=True, vmem_limit_bytes=60 * 2**20
        ),
    )(
        observed_count, direction.reshape(flat, nx), length_east, length_north,
        jnp.transpose(vertical_modes, (1, 0, 2)), amplitude,
        observed_cell.reshape(1, slots), observed_weight.reshape(1, slots),
        residual.reshape(flat, nx), increment.reshape(flat, nx), lanczos.reshape(K, flat, nx),
    )
    return tuple(out)


def solution(mesh):
    field = P(None, None, "row", "col")
    tile = P(("row", "col"))
    in_specs = (
        field, field, field, P(None, None, None, "row", "col"),
        P(), P(), P(), P(), tile, tile, tile,
    )
    return jax.shard_map(
        functools.partial(local, mesh.shape["row"], mesh.shape["col"]),
        mesh=mesh, in_specs=in_specs, out_specs=(field,) * 3, check_vma=False,
    )
```

```python
import functools

import jax
import jax.numpy as jnp
from jax import lax
from jax.experimental import pallas as pl
from jax.experimental.pallas import tpu as pltpu
from jax.sharding import PartitionSpec as P

MESH = pl.DeviceIdType.MESH
f32 = jnp.float32
bf16 = jnp.bfloat16
CHUNK = 32


def kernel(
    R, C, V, L, M, K, ny, nx, total_cells,
    cnt_ref, dir_hbm, len_e_hbm, len_n_hbm, vm_hbm, amp_hbm, cell_hbm, wgt_hbm,
    res_hbm, inc_hbm, lz_hbm,
    oinc_all, ores_all, odir_all,
    dir_ref, len_ref, vm_ref, amp_ref, cell_ref, wgt_ref,
    tab_ref, own_ref, near_ref, far_ref, mix_ref,
    res_ref, inc_ref, lz_ref,
    img_ref, lead_ref, mom_ref, hot_ref, wsum_ref,
    es_ref, er_ref, ns_ref, nr_ref, rs_ref, rr_ref,
    load_sem, e_ssem, e_rsem, n_ssem, n_rsem, r_ssem, r_rsem,
):
    N = R * C
    I = V * M
    oinc_ref, ores_ref, odir_ref = (
        x.reshape(V * L * ny, nx) for x in (oinc_all, ores_all, odir_all)
    )
    row, col = lax.axis_index("row"), lax.axis_index("col")
    me = row * C + col
    barrier = pltpu.get_barrier_semaphore()

    def place(d):
        peer = lax.rem(me + d, N)
        return (lax.div(peer, C), lax.rem(peer, C))

    def greet(d, carry):
        pl.semaphore_signal(barrier, inc=1, device_id=place(d), device_id_type=MESH)
        return carry

    plane = L * ny
    lead_rows = M * ny
    firsts = [
        pltpu.make_async_copy(len_e_hbm, len_ref.at[0], load_sem.at[3]),
        pltpu.make_async_copy(len_n_hbm, len_ref.at[1], load_sem.at[4]),
    ]
    others = [
        pltpu.make_async_copy(cell_hbm, cell_ref, load_sem.at[5]),
        pltpu.make_async_copy(wgt_hbm, wgt_ref, load_sem.at[6]),
        pltpu.make_async_copy(vm_hbm, vm_ref, load_sem.at[7]),
        pltpu.make_async_copy(amp_hbm, amp_ref, load_sem.at[8]),
    ]
    for v in range(V):
        part = pl.ds(v * plane, lead_rows)
        firsts.append(
            pltpu.make_async_copy(dir_hbm.at[part], dir_ref.at[part], load_sem.at[9 + v])
        )
        part = pl.ds(v * plane + lead_rows, plane - lead_rows)
        others.append(
            pltpu.make_async_copy(dir_hbm.at[part], dir_ref.at[part], load_sem.at[9 + V + v])
        )
    loads = [
        pltpu.make_async_copy(res_hbm, res_ref, load_sem.at[0]),
        pltpu.make_async_copy(lz_hbm, lz_ref, load_sem.at[1]),
        pltpu.make_async_copy(inc_hbm, inc_ref, load_sem.at[2]),
    ]
    for load in firsts + others + loads:
        load.start()
    lax.fori_loop(1, N, greet, 0)
    for load in firsts:
        load.wait()
    for i in range(I):
        v, m = i // M, i % M
        rows = slice(i * ny, (i + 1) * ny)
        for which, size in ((0, nx), (1, ny)):
            length = jnp.broadcast_to(len_ref[which, v : v + 1, m : m + 1], (ny, nx))
            tab_ref[which, rows, :] = -1.0 / (length * float(size))

    lane = lax.broadcasted_iota(jnp.int32, (1, 1, nx), 2)
    sub = lax.broadcasted_iota(jnp.int32, (1, ny, 1), 1)

    def log_alpha(which):
        return tab_ref[which].reshape(I, ny, nx)

    def scans(u, which):
        axis, size, at = ((2, nx, lane), (1, ny, sub))[which]
        power = jnp.exp(log_alpha(which))
        f, g = u, u
        shift = 1
        while shift < size:
            f = f + power * jnp.where(at >= shift, pltpu.roll(f, shift, axis), 0.0)
            g = g + power * jnp.where(at < size - shift, pltpu.roll(g, size - shift, axis), 0.0)
            power = power * power
            shift *= 2
        return f, g

    def weights(log_small, index, count, size):
        at = index.astype(f32)
        left, right, edge = [None], [None], []
        back = jnp.exp(log_small * (size * (float(count - 1) - at)))
        for d in range(count):
            wraps = d > index
            source = jnp.where(wraps, index - d + count, index - d).astype(f32)
            if d > 0:
                left.append(jnp.where(wraps, 0.0, jnp.exp(log_small * float(size * (d - 1)))))
                right.append(
                    jnp.where(wraps, jnp.exp(log_small * float(size * (count - d - 1))), 0.0)
                )
            edge.append(
                back * jnp.exp(log_small * (float(size * (count - 1)) - size * source + 1.0))
            )
        return left, right, edge

    def combine(table, own, received, copies):
        left_w, right_w, edge_w = table
        e, b, e_edge = own
        left = jnp.zeros_like(e)
        right = -edge_w[0] * e_edge
        for d, copy in enumerate(copies, 1):
            copy.wait_recv()
            e, b, e_edge = received(d)
            left += left_w[d] * e
            right += right_w[d] * b - edge_w[d] * e_edge
        for copy in copies:
            copy.wait_send()
        return left, right

    def tables(which):
        size, at = ((nx, lane), (ny, sub))[which]
        log_a = log_alpha(which)
        a = jnp.exp(log_a)
        scale = jnp.sqrt((1.0 - a) / (1.0 + a))
        at = at.astype(f32)
        own_ref[which] = scale.reshape(I * ny, nx)
        near_ref[which] = (scale * jnp.exp(log_a * (at + 1.0))).reshape(I * ny, nx)
        far_ref[which] = (scale * jnp.exp(log_a * (float(size) - at))).reshape(I * ny, nx)

    def east_copies(inst):
        return [
            pltpu.make_async_remote_copy(
                src_ref=es_ref.at[inst],
                dst_ref=er_ref.at[inst, d],
                send_sem=e_ssem.at[inst, d],
                recv_sem=e_rsem.at[inst, d],
                device_id=(row, lax.rem(col + d, C)),
                device_id_type=MESH,
            )
            for d in range(1, C)
        ]

    def north_copies(inst):
        return [
            pltpu.make_async_remote_copy(
                src_ref=ns_ref.at[inst],
                dst_ref=nr_ref.at[inst, d],
                send_sem=n_ssem.at[inst, d],
                recv_sem=n_rsem.at[inst, d],
                device_id=(lax.rem(row + d, R), col),
                device_id_type=MESH,
            )
            for d in range(1, R)
        ]

    small_lane = lax.broadcasted_iota(jnp.int32, (ny, nx), 1)

    def east_start(u, inst):
        f, g = scans(u, 0)
        first = jnp.zeros((ny, nx), f32)
        second = jnp.zeros((ny, nx), f32)
        for i in range(I):
            e = jnp.broadcast_to(f[i, :, nx - 1 : nx], (ny, nx))
            b = jnp.broadcast_to(g[i, :, 0:1], (ny, nx))
            first = jnp.where(small_lane == i, e, first)
            first = jnp.where(small_lane == I + i, b, first)
            second = jnp.where(small_lane == I + i, e, second)
        es_ref[inst, 0] = first
        es_ref[inst, 1] = second
        lead_ref[...] = (f + g - u).reshape(I * ny, nx)
        return east_copies(inst)

    def east_finish(inst, copies):
        left, right = combine(
            east_table,
            (es_ref[inst, 0], es_ref[inst, 0], es_ref[inst, 1]),
            lambda d: (er_ref[inst, d, 0], er_ref[inst, d, 0], er_ref[inst, d, 1]),
            copies,
        )
        for i in range(I):
            rows = slice(i * ny, (i + 1) * ny)
            x = jnp.broadcast_to(left[:, i : i + 1], (ny, nx))
            y = jnp.broadcast_to(right[:, I + i : I + i + 1], (ny, nx))
            lead_ref[rows, :] = (
                own_ref[0, rows, :] * lead_ref[rows, :]
                + near_ref[0, rows, :] * x
                + far_ref[0, rows, :] * y
            )

    def north_start(u, inst):
        f, g = scans(u, 1)
        mom_ref[0] = f.reshape(I * ny, nx)
        mom_ref[1] = g.reshape(I * ny, nx)
        ns_ref[inst, 0] = mom_ref[0, pl.ds(ny - 1, I, stride=ny), :]
        ns_ref[inst, 1] = mom_ref[1, pl.ds(0, I, stride=ny), :]
        lead_ref[...] = (f + g - u).reshape(I * ny, nx)
        return north_copies(inst)

    def north_finish(inst, copies):
        left, right = combine(
            north_table,
            (ns_ref[inst, 0], ns_ref[inst, 1], ns_ref[inst, 0]),
            lambda d: (nr_ref[inst, d, 0], nr_ref[inst, d, 1], nr_ref[inst, d, 0]),
            copies,
        )
        for i in range(I):
            rows = slice(i * ny, (i + 1) * ny)
            x = jnp.broadcast_to(left[i : i + 1, :], (ny, nx))
            y = jnp.broadcast_to(right[i : i + 1, :], (ny, nx))
            lead_ref[rows, :] = (
                own_ref[1, rows, :] * lead_ref[rows, :]
                + near_ref[1, rows, :] * x
                + far_ref[1, rows, :] * y
            )

    u = jnp.concatenate([dir_ref[v * plane : v * plane + M * ny, :] for v in range(V)], axis=0)
    copies = east_start(u.reshape(I, ny, nx), 0)
    pl.semaphore_wait(barrier, N - 1)
    for copy in copies:
        copy.start()

    log_small = jnp.zeros((ny, nx), f32)
    for i in range(I):
        hit = (small_lane == i) | (small_lane == I + i)
        log_small = jnp.where(hit, tab_ref[0, i * ny : (i + 1) * ny, :], log_small)
    east_table = weights(log_small, col, C, nx)
    tables(0)
    for load in others:
        load.wait()

    pad = mix_ref.shape[1] // 2
    cell = cell_ref[...]
    slots = cell.shape[1]
    level = lax.shift_right_logical(cell, (ny * nx).bit_length() - 1)
    spot = cell & (ny * nx - 1)
    hot_ref[...] = jnp.where(
        lax.broadcasted_iota(jnp.int32, (ny * nx, slots), 0) == spot, 1.0, 0.0
    ).astype(bf16)
    live = lax.broadcasted_iota(jnp.int32, (1, slots), 1) < cnt_ref[0]
    rest = jnp.where(live, wgt_ref[...], 0.0)
    at = lax.broadcasted_iota(jnp.int32, (pad, slots), 0)
    hits = [(at + v * L == level) & (at < L) for v in range(V)]
    lhs = []
    for _ in range(3):
        part = rest.astype(bf16).astype(f32)
        lhs += [jnp.where(hit, part, 0.0).astype(bf16) for hit in hits]
        rest = rest - part
    summed = lax.dot_general(
        jnp.concatenate(lhs, axis=0), hot_ref[...], (((1,), (1,)), ((), ())),
        preferred_element_type=f32,
    )
    for v in range(V):
        wsum_ref[v] = sum(
            summed[(n * V + v) * pad : (n * V + v + 1) * pad] for n in range(3)
        )
    mix_ref[...] = jnp.zeros_like(mix_ref)
    for v in range(V):
        mix_ref[v, 0:L, 0:L] = vm_ref[:, v, :] * amp_ref[v : v + 1, :]

    east_finish(0, copies)
    copies = north_start(lead_ref[...].reshape(I, ny, nx), 0)
    for copy in copies:
        copy.start()
    north_table = weights(tab_ref[1, pl.ds(0, I, stride=ny), :], row, R, ny)
    tables(1)

    def split(x):
        high = x.astype(bf16)
        return high, (x - high.astype(f32)).astype(bf16)

    def wide(x):
        high = x.astype(bf16).astype(f32)
        low = x - high
        return jnp.concatenate(
            [high + pltpu.roll(low, pad, 1), high], axis=1
        )[0:pad, :].astype(bf16)

    def tall(x):
        high, low = split(x)
        return jnp.concatenate([high, high, low, jnp.zeros_like(low)], axis=0)

    sides = []
    for v in range(V):
        mixed = mix_ref[v]
        sides.append((wide(mixed), wide(mixed.T)))
    north_finish(0, copies)

    spare = jnp.zeros((pad - L, nx), f32)
    for v in range(V):
        field = jnp.concatenate(
            [
                jnp.concatenate(
                    [
                        lead_ref[pl.ds(v * lead_rows + y, M, stride=ny), :],
                        dir_ref[pl.ds(v * plane + lead_rows + y, L - M, stride=ny), :],
                        spare,
                    ],
                    axis=0,
                )
                for y in range(ny)
            ],
            axis=1,
        )
        grid = jnp.dot(sides[v][0], tall(field), preferred_element_type=f32)
        back = jnp.dot(sides[v][1], tall(grid * wsum_ref[v]), preferred_element_type=f32)
        for y in range(ny):
            img_ref[pl.ds(v * plane + y, L, stride=ny), :] = back[0:L, y * nx : (y + 1) * nx]

    u = jnp.concatenate([img_ref[v * plane : v * plane + M * ny, :] for v in range(V)], axis=0)
    copies = north_start(u.reshape(I, ny, nx), 1)
    for copy in copies:
        copy.start()

    steps = V * plane // CHUNK

    def fold(x):
        return jnp.sum(x.reshape(CHUNK // 8, 8, nx), axis=0)

    loads[0].wait()
    loads[1].wait()
    zero = jnp.zeros((8, nx), f32)

    def first_dots(s, carry):
        rows = pl.ds(pl.multiple_of(s * CHUNK, CHUNK), CHUNK)
        r = res_ref[rows, :]
        out = [carry[0] + fold(r * r)]
        for k in range(K):
            out.append(carry[k + 1] + fold(r * lz_ref[k, rows, :].astype(f32)))
        return tuple(out)

    res_dots = lax.fori_loop(0, steps, first_dots, (zero,) * (K + 1))

    north_finish(1, copies)
    copies = east_start(lead_ref[...].reshape(I, ny, nx), 1)
    for copy in copies:
        copy.start()
    east_finish(1, copies)
    for v in range(V):
        img_ref[v * plane : v * plane + M * ny, :] = lead_ref[v * M * ny : (v + 1) * M * ny, :]

    def second_dots(s, carry):
        rows = pl.ds(pl.multiple_of(s * CHUNK, CHUNK), CHUNK)
        d = dir_ref[rows, :]
        image = d + img_ref[rows, :]
        img_ref[rows, :] = image
        out = [carry[0] + fold(d * image)]
        for k in range(K):
            out.append(carry[k + 1] + fold(image * lz_ref[k, rows, :].astype(f32)))
        return tuple(out)

    img_dots = lax.fori_loop(0, steps, second_dots, (zero,) * (K + 1))

    def reduce_copy(inst, over, along):
        return pltpu.make_async_remote_copy(
            src_ref=rs_ref.at[inst],
            dst_ref=rr_ref.at[inst, over * C + along],
            send_sem=r_ssem.at[inst],
            recv_sem=r_rsem.at[inst],
            device_id=(lax.rem(row + over, R), lax.rem(col + along, C)),
            device_id_type=MESH,
        )

    def reduce_start(inst):
        def go(over, carry):
            for along in range(C):
                reduce_copy(inst, over, along).start()
            return carry

        lax.fori_loop(1, R, go, 0)
        for along in range(1, C):
            reduce_copy(inst, 0, along).start()

    def reduce_finish(inst):
        every = pltpu.make_async_remote_copy(
            src_ref=rr_ref.at[inst, pl.ds(1, N - 1)],
            dst_ref=rr_ref.at[inst, pl.ds(1, N - 1)],
            send_sem=r_ssem.at[inst],
            recv_sem=r_rsem.at[inst],
            device_id=(row, lax.rem(col + 1, C)),
            device_id_type=MESH,
        )
        every.wait_recv()
        every.wait_send()
        rr_ref[inst, 0] = rs_ref[inst]
        return jnp.sum(rr_ref[inst], axis=0)

    sums = list(res_dots) + list(img_dots)
    small_sub = lax.broadcasted_iota(jnp.int32, (8, nx), 0)
    packed = zero
    for n, part in enumerate(sums):
        here = (small_sub == n % 8) & (small_lane == n // 8)
        packed = jnp.where(here, jnp.sum(part, axis=(0, 1), keepdims=True), packed)
    rs_ref[0] = packed
    reduce_start(0)
    loads[2].wait()
    totals = reduce_finish(0)

    def total(n):
        return totals[n % 8 : n % 8 + 1, n // 8 : n // 8 + 1]

    norm_old = total(0)
    step_size = norm_old / total(K + 1)
    coefficient = [
        jnp.broadcast_to((total(k + 1) - step_size * total(K + 2 + k)) / total_cells, (CHUNK, nx))
        for k in range(K)
    ]
    step_wide = jnp.broadcast_to(step_size, (CHUNK, nx))

    def update(s, carry):
        rows = pl.ds(pl.multiple_of(s * CHUNK, CHUNK), CHUNK)
        moved = res_ref[rows, :] - step_wide * img_ref[rows, :]
        for k in range(K):
            moved = moved - coefficient[k] * lz_ref[k, rows, :].astype(f32)
        ores_ref[rows, :] = moved
        return carry + fold(moved * moved)

    norm_part = lax.fori_loop(0, steps, update, zero)
    rs_ref[1] = jnp.broadcast_to(jnp.sum(norm_part, axis=(0, 1), keepdims=True), (8, nx))
    reduce_start(1)

    def advance(s, carry):
        rows = pl.ds(pl.multiple_of(s * CHUNK, CHUNK), CHUNK)
        oinc_ref[rows, :] = inc_ref[rows, :] + step_wide * dir_ref[rows, :]
        return carry

    lax.fori_loop(0, steps, advance, 0, unroll=4)
    ratio = jnp.broadcast_to(reduce_finish(1)[0:1, 0:1] / norm_old, (CHUNK, nx))

    def turn(s, carry):
        rows = pl.ds(pl.multiple_of(s * CHUNK, CHUNK), CHUNK)
        odir_ref[rows, :] = ores_ref[rows, :] + ratio * dir_ref[rows, :]
        return carry

    lax.fori_loop(0, steps, turn, 0, unroll=4)


def local(
    R, C,
    increment, residual, direction, lanczos, vertical_modes, amplitude,
    length_east, length_north, observed_cell, observed_weight, observed_count,
):
    V, L, ny, nx = direction.shape
    M = length_east.shape[1]
    K = lanczos.shape[0]
    I = V * M
    N = R * C
    flat = V * L * ny
    slots = observed_cell.shape[0]
    pad = (L + 15) // 16 * 16
    hbm = pl.BlockSpec(memory_space=pltpu.HBM)
    smem = pl.BlockSpec(memory_space=pltpu.SMEM)
    field = pltpu.VMEM((V, L, ny, nx), f32)
    near = pl.BlockSpec(memory_space=pltpu.VMEM)
    big = pltpu.VMEM((flat, nx), f32)
    out = pl.pallas_call(
        functools.partial(kernel, R, C, V, L, M, K, ny, nx, float(flat * nx * N)),
        out_shape=(field,) * 3,
        in_specs=[smem] + [hbm] * 10,
        out_specs=(near,) * 3,
        scratch_shapes=[
            big, pltpu.VMEM((2, V, M), f32), pltpu.VMEM((L, V, L), f32),
            pltpu.VMEM((V, L), f32), pltpu.VMEM((1, slots), jnp.int32), pltpu.VMEM((1, slots), f32),
            pltpu.VMEM((2, I * ny, nx), f32), pltpu.VMEM((2, I * ny, nx), f32),
            pltpu.VMEM((2, I * ny, nx), f32), pltpu.VMEM((2, I * ny, nx), f32),
            pltpu.VMEM((V, 2 * pad, 2 * pad), f32),
            big, big, pltpu.VMEM((K, flat, nx), bf16),
            big, pltpu.VMEM((I * ny, nx), f32), pltpu.VMEM((2, I * ny, nx), f32),
            pltpu.VMEM((ny * nx, slots), bf16), pltpu.VMEM((V, pad, ny * nx), f32),
            pltpu.VMEM((2, 2, ny, nx), f32), pltpu.VMEM((2, C, 2, ny, nx), f32),
            pltpu.VMEM((2, 2, I, nx), f32), pltpu.VMEM((2, R, 2, I, nx), f32),
            pltpu.VMEM((2, 8, nx), f32), pltpu.VMEM((2, N, 8, nx), f32),
            pltpu.SemaphoreType.DMA((9 + 2 * V,)),
            pltpu.SemaphoreType.DMA((2, C)), pltpu.SemaphoreType.DMA((2, C)),
            pltpu.SemaphoreType.DMA((2, R)), pltpu.SemaphoreType.DMA((2, R)),
            pltpu.SemaphoreType.DMA((2,)), pltpu.SemaphoreType.DMA((2,)),
        ],
        compiler_params=pltpu.CompilerParams(
            collective_id=0, has_side_effects=True, vmem_limit_bytes=60 * 2**20
        ),
    )(
        observed_count, direction.reshape(flat, nx), length_east, length_north,
        jnp.transpose(vertical_modes, (1, 0, 2)), amplitude,
        observed_cell.reshape(1, slots), observed_weight.reshape(1, slots),
        residual.reshape(flat, nx), increment.reshape(flat, nx), lanczos.reshape(K, flat, nx),
    )
    return tuple(out)


def solution(mesh):
    field = P(None, None, "row", "col")
    tile = P(("row", "col"))
    in_specs = (
        field, field, field, P(None, None, None, "row", "col"),
        P(), P(), P(), P(), tile, tile, tile,
    )
    return jax.shard_map(
        functools.partial(local, mesh.shape["row"], mesh.shape["col"]),
        mesh=mesh, in_specs=in_specs, out_specs=(field,) * 3, check_vma=False,
    )
```

```python
import functools

import jax
import jax.numpy as jnp
from jax import lax
from jax.experimental import pallas as pl
from jax.experimental.pallas import tpu as pltpu
from jax.sharding import PartitionSpec as P

MESH = pl.DeviceIdType.MESH
f32 = jnp.float32
bf16 = jnp.bfloat16
CHUNK = 32


def kernel(
    R, C, V, L, M, K, ny, nx, total_cells,
    cnt_ref, dir_hbm, len_e_hbm, len_n_hbm, vm_hbm, amp_hbm, cell_hbm, wgt_hbm,
    res_hbm, inc_hbm, lz_hbm,
    oinc_all, ores_all, odir_all,
    dir_ref, len_ref, vm_ref, amp_ref, cell_ref, wgt_ref,
    tab_ref, own_ref, near_ref, far_ref, mix_ref,
    res_ref, inc_ref, lz_ref,
    img_ref, lead_ref, mom_ref, hot_ref, wsum_ref,
    es_ref, er_ref, ns_ref, nr_ref, rs_ref, rr_ref,
    load_sem, e_ssem, e_rsem, n_ssem, n_rsem, r_ssem, r_rsem,
):
    N = R * C
    I = V * M
    oinc_ref, ores_ref, odir_ref = (
        x.reshape(V * L * ny, nx) for x in (oinc_all, ores_all, odir_all)
    )
    row, col = lax.axis_index("row"), lax.axis_index("col")
    me = row * C + col
    barrier = pltpu.get_barrier_semaphore()

    def place(d):
        peer = lax.rem(me + d, N)
        return (lax.div(peer, C), lax.rem(peer, C))

    def greet(d, carry):
        pl.semaphore_signal(barrier, inc=1, device_id=place(d), device_id_type=MESH)
        return carry

    plane = L * ny
    lead_rows = M * ny
    firsts = [
        pltpu.make_async_copy(len_e_hbm, len_ref.at[0], load_sem.at[3]),
        pltpu.make_async_copy(len_n_hbm, len_ref.at[1], load_sem.at[4]),
    ]
    others = [
        pltpu.make_async_copy(cell_hbm, cell_ref, load_sem.at[5]),
        pltpu.make_async_copy(wgt_hbm, wgt_ref, load_sem.at[6]),
        pltpu.make_async_copy(vm_hbm, vm_ref, load_sem.at[7]),
        pltpu.make_async_copy(amp_hbm, amp_ref, load_sem.at[8]),
    ]
    for v in range(V):
        part = pl.ds(v * plane, lead_rows)
        firsts.append(
            pltpu.make_async_copy(dir_hbm.at[part], dir_ref.at[part], load_sem.at[9 + v])
        )
        part = pl.ds(v * plane + lead_rows, plane - lead_rows)
        others.append(
            pltpu.make_async_copy(dir_hbm.at[part], dir_ref.at[part], load_sem.at[9 + V + v])
        )
    loads = [
        pltpu.make_async_copy(res_hbm, res_ref, load_sem.at[0]),
        pltpu.make_async_copy(lz_hbm, lz_ref, load_sem.at[1]),
        pltpu.make_async_copy(inc_hbm, inc_ref, load_sem.at[2]),
    ]
    for load in firsts + others + loads:
        load.start()
    lax.fori_loop(1, N, greet, 0)
    for load in firsts:
        load.wait()
    for i in range(I):
        v, m = i // M, i % M
        rows = slice(i * ny, (i + 1) * ny)
        for which, size in ((0, nx), (1, ny)):
            length = jnp.broadcast_to(len_ref[which, v : v + 1, m : m + 1], (ny, nx))
            tab_ref[which, rows, :] = -1.0 / (length * float(size))

    lane = lax.broadcasted_iota(jnp.int32, (1, 1, nx), 2)
    sub = lax.broadcasted_iota(jnp.int32, (1, ny, 1), 1)

    def log_alpha(which):
        return tab_ref[which].reshape(I, ny, nx)

    def scans(u, which):
        axis, size, at = ((2, nx, lane), (1, ny, sub))[which]
        power = jnp.exp(log_alpha(which))
        f, g = u, u
        shift = 1
        while shift < size:
            f = f + power * jnp.where(at >= shift, pltpu.roll(f, shift, axis), 0.0)
            g = g + power * jnp.where(at < size - shift, pltpu.roll(g, size - shift, axis), 0.0)
            power = power * power
            shift *= 2
        return f, g

    def weights(log_small, index, count, size):
        at = index.astype(f32)
        left, right, edge = [None], [None], []
        back = jnp.exp(log_small * (size * (float(count - 1) - at)))
        for d in range(count):
            wraps = d > index
            source = jnp.where(wraps, index - d + count, index - d).astype(f32)
            if d > 0:
                left.append(jnp.where(wraps, 0.0, jnp.exp(log_small * float(size * (d - 1)))))
                right.append(
                    jnp.where(wraps, jnp.exp(log_small * float(size * (count - d - 1))), 0.0)
                )
            edge.append(
                back * jnp.exp(log_small * (float(size * (count - 1)) - size * source + 1.0))
            )
        return left, right, edge

    def combine(table, own, received, copies):
        left_w, right_w, edge_w = table
        e, b, e_edge = own
        left = jnp.zeros_like(e)
        right = -edge_w[0] * e_edge
        for d, copy in enumerate(copies, 1):
            copy.wait_recv()
            e, b, e_edge = received(d)
            left += left_w[d] * e
            right += right_w[d] * b - edge_w[d] * e_edge
        for copy in copies:
            copy.wait_send()
        return left, right

    def tables(which):
        size, at = ((nx, lane), (ny, sub))[which]
        log_a = log_alpha(which)
        a = jnp.exp(log_a)
        scale = jnp.sqrt((1.0 - a) / (1.0 + a))
        at = at.astype(f32)
        own_ref[which] = scale.reshape(I * ny, nx)
        near_ref[which] = (scale * jnp.exp(log_a * (at + 1.0))).reshape(I * ny, nx)
        far_ref[which] = (scale * jnp.exp(log_a * (float(size) - at))).reshape(I * ny, nx)

    def east_copies(inst):
        return [
            pltpu.make_async_remote_copy(
                src_ref=es_ref.at[inst],
                dst_ref=er_ref.at[inst, d],
                send_sem=e_ssem.at[inst, d],
                recv_sem=e_rsem.at[inst, d],
                device_id=(row, lax.rem(col + d, C)),
                device_id_type=MESH,
            )
            for d in range(1, C)
        ]

    def north_copies(inst):
        return [
            pltpu.make_async_remote_copy(
                src_ref=ns_ref.at[inst],
                dst_ref=nr_ref.at[inst, d],
                send_sem=n_ssem.at[inst, d],
                recv_sem=n_rsem.at[inst, d],
                device_id=(lax.rem(row + d, R), col),
                device_id_type=MESH,
            )
            for d in range(1, R)
        ]

    small_lane = lax.broadcasted_iota(jnp.int32, (ny, nx), 1)

    def east_start(u, inst):
        f, g = scans(u, 0)
        first = jnp.zeros((ny, nx), f32)
        second = jnp.zeros((ny, nx), f32)
        for i in range(I):
            e = jnp.broadcast_to(f[i, :, nx - 1 : nx], (ny, nx))
            b = jnp.broadcast_to(g[i, :, 0:1], (ny, nx))
            first = jnp.where(small_lane == i, e, first)
            first = jnp.where(small_lane == I + i, b, first)
            second = jnp.where(small_lane == I + i, e, second)
        es_ref[inst, 0] = first
        es_ref[inst, 1] = second
        lead_ref[...] = (f + g - u).reshape(I * ny, nx)
        return east_copies(inst)

    def east_finish(inst, copies):
        left, right = combine(
            east_table,
            (es_ref[inst, 0], es_ref[inst, 0], es_ref[inst, 1]),
            lambda d: (er_ref[inst, d, 0], er_ref[inst, d, 0], er_ref[inst, d, 1]),
            copies,
        )
        for i in range(I):
            rows = slice(i * ny, (i + 1) * ny)
            x = jnp.broadcast_to(left[:, i : i + 1], (ny, nx))
            y = jnp.broadcast_to(right[:, I + i : I + i + 1], (ny, nx))
            lead_ref[rows, :] = (
                own_ref[0, rows, :] * lead_ref[rows, :]
                + near_ref[0, rows, :] * x
                + far_ref[0, rows, :] * y
            )

    def north_start(u, inst):
        f, g = scans(u, 1)
        mom_ref[0] = f.reshape(I * ny, nx)
        mom_ref[1] = g.reshape(I * ny, nx)
        ns_ref[inst, 0] = mom_ref[0, pl.ds(ny - 1, I, stride=ny), :]
        ns_ref[inst, 1] = mom_ref[1, pl.ds(0, I, stride=ny), :]
        lead_ref[...] = (f + g - u).reshape(I * ny, nx)
        return north_copies(inst)

    def north_finish(inst, copies):
        left, right = combine(
            north_table,
            (ns_ref[inst, 0], ns_ref[inst, 1], ns_ref[inst, 0]),
            lambda d: (nr_ref[inst, d, 0], nr_ref[inst, d, 1], nr_ref[inst, d, 0]),
            copies,
        )
        for i in range(I):
            rows = slice(i * ny, (i + 1) * ny)
            x = jnp.broadcast_to(left[i : i + 1, :], (ny, nx))
            y = jnp.broadcast_to(right[i : i + 1, :], (ny, nx))
            lead_ref[rows, :] = (
                own_ref[1, rows, :] * lead_ref[rows, :]
                + near_ref[1, rows, :] * x
                + far_ref[1, rows, :] * y
            )

    u = jnp.concatenate([dir_ref[v * plane : v * plane + M * ny, :] for v in range(V)], axis=0)
    copies = east_start(u.reshape(I, ny, nx), 0)
    pl.semaphore_wait(barrier, N - 1)
    for copy in copies:
        copy.start()

    log_small = jnp.zeros((ny, nx), f32)
    for i in range(I):
        hit = (small_lane == i) | (small_lane == I + i)
        log_small = jnp.where(hit, tab_ref[0, i * ny : (i + 1) * ny, :], log_small)
    east_table = weights(log_small, col, C, nx)
    tables(0)
    for load in others:
        load.wait()

    pad = mix_ref.shape[1] // 2
    cell = cell_ref[...]
    slots = cell.shape[1]
    level = lax.shift_right_logical(cell, (ny * nx).bit_length() - 1)
    spot = cell & (ny * nx - 1)
    hot_ref[...] = jnp.where(
        lax.broadcasted_iota(jnp.int32, (ny * nx, slots), 0) == spot, 1.0, 0.0
    ).astype(bf16)
    live = lax.broadcasted_iota(jnp.int32, (1, slots), 1) < cnt_ref[0]
    rest = jnp.where(live, wgt_ref[...], 0.0)
    at = lax.broadcasted_iota(jnp.int32, (pad, slots), 0)
    hits = [(at + v * L == level) & (at < L) for v in range(V)]
    lhs = []
    for _ in range(3):
        part = rest.astype(bf16).astype(f32)
        lhs += [jnp.where(hit, part, 0.0).astype(bf16) for hit in hits]
        rest = rest - part
    summed = lax.dot_general(
        jnp.concatenate(lhs, axis=0), hot_ref[...], (((1,), (1,)), ((), ())),
        preferred_element_type=f32,
    )
    for v in range(V):
        wsum_ref[v] = sum(
            summed[(n * V + v) * pad : (n * V + v + 1) * pad] for n in range(3)
        )
    mix_ref[...] = jnp.zeros_like(mix_ref)
    for v in range(V):
        mix_ref[v, 0:L, 0:L] = vm_ref[:, v, :] * amp_ref[v : v + 1, :]

    east_finish(0, copies)
    copies = north_start(lead_ref[...].reshape(I, ny, nx), 0)
    for copy in copies:
        copy.start()
    north_table = weights(tab_ref[1, pl.ds(0, I, stride=ny), :], row, R, ny)
    tables(1)

    def split(x):
        high = x.astype(bf16)
        return high, (x - high.astype(f32)).astype(bf16)

    def wide(x):
        high = x.astype(bf16).astype(f32)
        low = x - high
        return jnp.concatenate(
            [high + pltpu.roll(low, pad, 1), high], axis=1
        )[0:pad, :].astype(bf16)

    def tall(x):
        high, low = split(x)
        return jnp.concatenate([high, high, low, jnp.zeros_like(low)], axis=0)

    sides = []
    for v in range(V):
        mixed = mix_ref[v]
        sides.append((wide(mixed), wide(mixed.T)))
    north_finish(0, copies)

    spare = jnp.zeros((pad - L, nx), f32)
    for v in range(V):
        field = jnp.concatenate(
            [
                jnp.concatenate(
                    [
                        lead_ref[pl.ds(v * lead_rows + y, M, stride=ny), :],
                        dir_ref[pl.ds(v * plane + lead_rows + y, L - M, stride=ny), :],
                        spare,
                    ],
                    axis=0,
                )
                for y in range(ny)
            ],
            axis=1,
        )
        grid = jnp.dot(sides[v][0], tall(field), preferred_element_type=f32)
        back = jnp.dot(sides[v][1], tall(grid * wsum_ref[v]), preferred_element_type=f32)
        for y in range(ny):
            img_ref[pl.ds(v * plane + y, L, stride=ny), :] = back[0:L, y * nx : (y + 1) * nx]

    u = jnp.concatenate([img_ref[v * plane : v * plane + M * ny, :] for v in range(V)], axis=0)
    copies = north_start(u.reshape(I, ny, nx), 1)
    for copy in copies:
        copy.start()

    steps = V * plane // CHUNK

    def fold(x):
        return jnp.sum(x.reshape(CHUNK // 8, 8, nx), axis=0)

    loads[0].wait()
    loads[1].wait()
    zero = jnp.zeros((8, nx), f32)

    def first_dots(s, carry):
        rows = pl.ds(pl.multiple_of(s * CHUNK, CHUNK), CHUNK)
        r = res_ref[rows, :]
        out = [carry[0] + fold(r * r)]
        for k in range(K):
            out.append(carry[k + 1] + fold(r * lz_ref[k, rows, :].astype(f32)))
        return tuple(out)

    res_dots = lax.fori_loop(0, steps, first_dots, (zero,) * (K + 1))

    north_finish(1, copies)
    copies = east_start(lead_ref[...].reshape(I, ny, nx), 1)
    for copy in copies:
        copy.start()
    east_finish(1, copies)
    for v in range(V):
        img_ref[v * plane : v * plane + M * ny, :] = lead_ref[v * M * ny : (v + 1) * M * ny, :]

    def second_dots(s, carry):
        rows = pl.ds(pl.multiple_of(s * CHUNK, CHUNK), CHUNK)
        d = dir_ref[rows, :]
        image = d + img_ref[rows, :]
        img_ref[rows, :] = image
        out = [carry[0] + fold(d * image)]
        for k in range(K):
            out.append(carry[k + 1] + fold(image * lz_ref[k, rows, :].astype(f32)))
        return tuple(out)

    img_dots = lax.fori_loop(0, steps, second_dots, (zero,) * (K + 1), unroll=2)

    def reduce_copy(inst, over, along):
        return pltpu.make_async_remote_copy(
            src_ref=rs_ref.at[inst],
            dst_ref=rr_ref.at[inst, over * C + along],
            send_sem=r_ssem.at[inst],
            recv_sem=r_rsem.at[inst],
            device_id=(lax.rem(row + over, R), lax.rem(col + along, C)),
            device_id_type=MESH,
        )

    def reduce_start(inst):
        def go(over, carry):
            for along in range(C):
                reduce_copy(inst, over, along).start()
            return carry

        lax.fori_loop(1, R, go, 0)
        for along in range(1, C):
            reduce_copy(inst, 0, along).start()

    def reduce_finish(inst):
        every = pltpu.make_async_remote_copy(
            src_ref=rr_ref.at[inst, pl.ds(1, N - 1)],
            dst_ref=rr_ref.at[inst, pl.ds(1, N - 1)],
            send_sem=r_ssem.at[inst],
            recv_sem=r_rsem.at[inst],
            device_id=(row, lax.rem(col + 1, C)),
            device_id_type=MESH,
        )
        every.wait_recv()
        every.wait_send()
        rr_ref[inst, 0] = rs_ref[inst]
        return jnp.sum(rr_ref[inst], axis=0)

    sums = list(res_dots) + list(img_dots)
    small_sub = lax.broadcasted_iota(jnp.int32, (8, nx), 0)
    packed = zero
    for n, part in enumerate(sums):
        here = (small_sub == n % 8) & (small_lane == n // 8)
        packed = jnp.where(here, jnp.sum(part, axis=(0, 1), keepdims=True), packed)
    rs_ref[0] = packed
    reduce_start(0)
    loads[2].wait()
    totals = reduce_finish(0)

    def total(n):
        return totals[n % 8 : n % 8 + 1, n // 8 : n // 8 + 1]

    norm_old = total(0)
    step_size = norm_old / total(K + 1)
    coefficient = [
        jnp.broadcast_to((total(k + 1) - step_size * total(K + 2 + k)) / total_cells, (CHUNK, nx))
        for k in range(K)
    ]
    step_wide = jnp.broadcast_to(step_size, (CHUNK, nx))

    def update(s, carry):
        rows = pl.ds(pl.multiple_of(s * CHUNK, CHUNK), CHUNK)
        moved = res_ref[rows, :] - step_wide * img_ref[rows, :]
        for k in range(K):
            moved = moved - coefficient[k] * lz_ref[k, rows, :].astype(f32)
        ores_ref[rows, :] = moved
        return carry + fold(moved * moved)

    norm_part = lax.fori_loop(0, steps, update, zero, unroll=2)
    rs_ref[1] = jnp.broadcast_to(jnp.sum(norm_part, axis=(0, 1), keepdims=True), (8, nx))
    reduce_start(1)

    def advance(s, carry):
        rows = pl.ds(pl.multiple_of(s * CHUNK, CHUNK), CHUNK)
        oinc_ref[rows, :] = inc_ref[rows, :] + step_wide * dir_ref[rows, :]
        return carry

    lax.fori_loop(0, steps, advance, 0, unroll=4)
    ratio = jnp.broadcast_to(reduce_finish(1)[0:1, 0:1] / norm_old, (CHUNK, nx))

    def turn(s, carry):
        rows = pl.ds(pl.multiple_of(s * CHUNK, CHUNK), CHUNK)
        odir_ref[rows, :] = ores_ref[rows, :] + ratio * dir_ref[rows, :]
        return carry

    lax.fori_loop(0, steps, turn, 0, unroll=4)


def local(
    R, C,
    increment, residual, direction, lanczos, vertical_modes, amplitude,
    length_east, length_north, observed_cell, observed_weight, observed_count,
):
    V, L, ny, nx = direction.shape
    M = length_east.shape[1]
    K = lanczos.shape[0]
    I = V * M
    N = R * C
    flat = V * L * ny
    slots = observed_cell.shape[0]
    pad = (L + 15) // 16 * 16
    hbm = pl.BlockSpec(memory_space=pltpu.HBM)
    smem = pl.BlockSpec(memory_space=pltpu.SMEM)
    field = pltpu.VMEM((V, L, ny, nx), f32)
    near = pl.BlockSpec(memory_space=pltpu.VMEM)
    big = pltpu.VMEM((flat, nx), f32)
    out = pl.pallas_call(
        functools.partial(kernel, R, C, V, L, M, K, ny, nx, float(flat * nx * N)),
        out_shape=(field,) * 3,
        in_specs=[smem] + [hbm] * 10,
        out_specs=(near,) * 3,
        scratch_shapes=[
            big, pltpu.VMEM((2, V, M), f32), pltpu.VMEM((L, V, L), f32),
            pltpu.VMEM((V, L), f32), pltpu.VMEM((1, slots), jnp.int32), pltpu.VMEM((1, slots), f32),
            pltpu.VMEM((2, I * ny, nx), f32), pltpu.VMEM((2, I * ny, nx), f32),
            pltpu.VMEM((2, I * ny, nx), f32), pltpu.VMEM((2, I * ny, nx), f32),
            pltpu.VMEM((V, 2 * pad, 2 * pad), f32),
            big, big, pltpu.VMEM((K, flat, nx), bf16),
            big, pltpu.VMEM((I * ny, nx), f32), pltpu.VMEM((2, I * ny, nx), f32),
            pltpu.VMEM((ny * nx, slots), bf16), pltpu.VMEM((V, pad, ny * nx), f32),
            pltpu.VMEM((2, 2, ny, nx), f32), pltpu.VMEM((2, C, 2, ny, nx), f32),
            pltpu.VMEM((2, 2, I, nx), f32), pltpu.VMEM((2, R, 2, I, nx), f32),
            pltpu.VMEM((2, 8, nx), f32), pltpu.VMEM((2, N, 8, nx), f32),
            pltpu.SemaphoreType.DMA((9 + 2 * V,)),
            pltpu.SemaphoreType.DMA((2, C)), pltpu.SemaphoreType.DMA((2, C)),
            pltpu.SemaphoreType.DMA((2, R)), pltpu.SemaphoreType.DMA((2, R)),
            pltpu.SemaphoreType.DMA((2,)), pltpu.SemaphoreType.DMA((2,)),
        ],
        compiler_params=pltpu.CompilerParams(
            collective_id=0, has_side_effects=True, vmem_limit_bytes=60 * 2**20
        ),
    )(
        observed_count, direction.reshape(flat, nx), length_east, length_north,
        jnp.transpose(vertical_modes, (1, 0, 2)), amplitude,
        observed_cell.reshape(1, slots), observed_weight.reshape(1, slots),
        residual.reshape(flat, nx), increment.reshape(flat, nx), lanczos.reshape(K, flat, nx),
    )
    return tuple(out)


def solution(mesh):
    field = P(None, None, "row", "col")
    tile = P(("row", "col"))
    in_specs = (
        field, field, field, P(None, None, None, "row", "col"),
        P(), P(), P(), P(), tile, tile, tile,
    )
    return jax.shard_map(
        functools.partial(local, mesh.shape["row"], mesh.shape["col"]),
        mesh=mesh, in_specs=in_specs, out_specs=(field,) * 3, check_vma=False,
    )
```
